512 devices in a mesh: sub: 128 (over y, z, core), grp: 4 (over x).
Axes of the slice: x: 4, y: 8, z: 8, core: 2. Of those that a mesh axis runs over, the one named last changes fastest.
Arguments:
- deflation: bfloat16 [512, 512, 4, 128], P(None, 'sub', 'grp'), may hold values from -0.045643546 to 0.045643546
- shift_field: float32 [512, 4, 128], P('sub', 'grp'), may hold values from 0.5 to 8
- counts: int32 [128], P('sub'), may hold values from 128 to 512, as said below
- right_sides: float32 [65536, 256], P(('sub', 'grp')), may hold values from -6 to 6
Outputs:
- coarse_solution: float32 [65536, 256], P(('sub', 'grp'))
The draws below stay inside these ranges and needn't reach their ends.
Inputs may be any that keep to these rules, and one draw needn't show every extreme that they name: `counts`: live deflation vectors of each subdomain; some subdomain has 512 and some 512 // 4.
All inputs are finite; a program needn't handle non-finite values.
Results may differ from the reference program's by a relative error of at most 0.0014.
Values may be sent and summed in bfloat16 or wider, within the bound.
No kernel may reach another device: no remote copies, remote signals or barrier semaphores. Data moves between devices by JAX's collectives and lax.ppermute only.
A program may use at most 64 MiB of HBM per device.

```python
import math
import jax
import jax.numpy as jnp
from jax import lax

KMAX = 512
CZ = 4
CX = 128
NRHS = 256
SWEEPS = 6
SUBS = 128
BLK = 128
NZ = 512
NY = 4
N_GRP = 4


def draw_deflation(key, part):
    key_common = jax.random.fold_in(key, 11)
    key_noise = jax.random.fold_in(key, 12)
    shape = (KMAX, NZ, NY, CX)
    common = 0.7 * jax.random.normal(key_common, (KMAX, 1, 1, 1), jnp.float32)
    noise = jax.random.normal(key_noise, shape, jnp.float32)
    values = jnp.clip(common + noise, -8.0, 8.0) / jnp.sqrt(15.0 * CZ * NY * CX)
    return values.astype(jnp.bfloat16)


def draw_counts(key, part):
    key_values = jax.random.fold_in(key, 21)
    key_high = jax.random.fold_in(key, 22)
    key_low = jax.random.fold_in(key, 23)
    values = jax.random.randint(key_values, (SUBS,), KMAX // 4, KMAX + 1, jnp.int32)
    high_index = jax.random.randint(key_high, (), 0, SUBS, jnp.int32)
    step_over = jax.random.randint(key_low, (), 1, SUBS, jnp.int32)
    low_index = (high_index + step_over) % SUBS
    values = values.at[high_index].set(KMAX)
    values = values.at[low_index].set(KMAX // 4)
    return values


def level_of(stream_key, dims, cuts, smallest, top_value):
    def one(axis_at, parts):
        draws = jax.random.uniform(jax.random.fold_in(jax.random.fold_in(stream_key, 6), axis_at), (parts,), jnp.float32, smallest / len(cuts), top_value / len(cuts))
        return jnp.repeat(jnp.exp(draws), dims[axis_at] // parts).reshape((-1,) + (1,) * (len(dims) - axis_at - 1))

    level = one(*cuts[0])
    for cut in cuts[1:]:
        level = level * one(*cut)
    return level


def bell_draw(key, extent, scale, reach, pieces=(), held_as=jnp.bfloat16):
    gain = level_of(key, extent, pieces, -0.22, 0.18) if pieces else 1.0
    values = jax.random.normal(key, extent, jnp.float32) * scale * gain
    return jnp.minimum(jnp.maximum(values, -reach), reach).astype(held_as)


def setup_inputs(seed: int = 0) -> dict:
    arg_keys = jax.random.split(jax.random.key(seed), 5)
    deflation = draw_deflation(jax.random.fold_in(arg_keys[4], 71), 0)
    shift_field = jnp.clip(jnp.exp(math.log(8.0) - 2.7725887 * jax.random.uniform(arg_keys[1], (NZ, NY, CX), jnp.float32) ** level_of(arg_keys[1], (NZ, NY, CX), ((0, 128), (1, 4)), -0.2, 0.2)), 0.5, 8.0)
    counts = draw_counts(jax.random.fold_in(arg_keys[4], 71), 0)
    right_sides = bell_draw(arg_keys[3], (SUBS * KMAX, NRHS), 1.0, 6.0, ((0, 512),), jnp.float32)
    return dict(deflation=deflation, shift_field=shift_field, counts=counts, right_sides=right_sides)


damping = 0.7

def smooth_last(values):
    width_x = values.shape[-1]
    positions = lax.iota(jnp.int32, width_x)
    left_side = jnp.where(positions >= 1, jnp.roll(values, 1, axis=-1), 0.0)
    right_side = jnp.where(positions < width_x - 1, jnp.roll(values, -1, axis=-1), 0.0)
    return values + 0.5 * (left_side + right_side)

def smooth_valid(values, which_axis):
    length = values.shape[which_axis]
    center = lax.slice_in_dim(values, 1, length - 1, axis=which_axis)
    lower = lax.slice_in_dim(values, 0, length - 2, axis=which_axis)
    upper = lax.slice_in_dim(values, 2, length, axis=which_axis)
    return center + 0.5 * (lower + upper)

def pad_axis(values, which_axis):
    widths = [(0, 0)] * values.ndim
    widths[which_axis] = (1, 1)
    return jnp.pad(values, widths)

def contract(left_part, right_part):
    return lax.dot_general(left_part.astype(jnp.float32), right_part.astype(jnp.float32), (((1,), (1,)), ((), ())), preferred_element_type=jnp.float32)

def reference(deflation, shift_field, counts, right_sides):
    slot_ids = lax.iota(jnp.int32, KMAX)

    def neighbour_plane(other, plane):
        valid = (other >= 0) & (other < SUBS)
        safe = jnp.clip(other, 0, SUBS - 1)
        plane_index = jnp.clip(plane, 0, NZ - 1).astype(jnp.int32)
        values = lax.dynamic_slice_in_dim(deflation, plane_index, 1, 1)[:, 0]
        live_other = (slot_ids < counts[safe]) & valid
        values = jnp.where(live_other[:, None, None], values, jnp.zeros((), deflation.dtype))
        along = smooth_valid(pad_axis(smooth_last(values.astype(jnp.float32)), 1), 1)
        return along.astype(jnp.bfloat16).reshape(KMAX, -1)

    def slab_rows(slab):
        begin = (slab * CZ).astype(jnp.int32)
        values = lax.dynamic_slice_in_dim(deflation, begin, CZ, 1)
        live_slots = slot_ids < counts[slab]
        masked = jnp.where(live_slots[:, None, None, None], values, jnp.zeros((), deflation.dtype))
        shift_slab = lax.dynamic_slice_in_dim(shift_field, begin, CZ, 0)
        own_field = masked.astype(jnp.float32)
        along_x = smooth_last(own_field)
        along_y = smooth_valid(pad_axis(along_x, 2), 2)
        along_z = smooth_valid(pad_axis(along_y, 1), 1)
        images = ((16.0 + shift_slab) * own_field - 2.0 * along_z).astype(jnp.bfloat16)
        above_plane = neighbour_plane(slab + 1, (slab + 1) * CZ)
        below_plane = neighbour_plane(slab - 1, slab * CZ - 1)
        top_plane = masked[:, CZ - 1].reshape(KMAX, -1)
        bottom = masked[:, 0].reshape(KMAX, -1)
        lower_part = -contract(bottom, below_plane)
        middle = contract(masked.reshape(KMAX, -1), images.reshape(KMAX, -1))
        upper_part = -contract(top_plane, above_plane)
        coarse = jnp.concatenate([lower_part, middle, upper_part], axis=1)
        columns = lax.iota(jnp.int32, 3 * KMAX)
        pad_mask = (columns[None, :] == slot_ids[:, None] + KMAX) & jnp.logical_not(live_slots)[:, None]
        return coarse + jnp.where(pad_mask, 1.0, 0.0).astype(jnp.float32)
    coarse = lax.map(slab_rows, jnp.arange(SUBS, dtype=jnp.int32))
    middle = coarse[:, :, KMAX:2 * KMAX]
    blocks = jnp.stack([middle[:, g * BLK:(g + 1) * BLK, g * BLK:(g + 1) * BLK] for g in range(N_GRP)], axis=1)
    factors = jnp.linalg.cholesky(blocks)

    def solve_one(factor, values):
        return jax.scipy.linalg.cho_solve((factor, True), values)
    solve_all = jax.vmap(jax.vmap(solve_one))
    live_rows = slot_ids[None, :] < counts[:, None]
    rhs = right_sides.reshape(SUBS, KMAX, NRHS)
    rhs = jnp.where(live_rows[:, :, None], rhs, 0.0)
    current = damping * solve_all(factors, rhs.reshape(SUBS, N_GRP, BLK, NRHS)).reshape(SUBS, KMAX, NRHS)
    zeros = jnp.zeros((1, KMAX, NRHS), jnp.float32)
    for sweep in range(SWEEPS - 1):
        lower_iter = jnp.concatenate([zeros, current[:-1]], axis=0)
        upper_iter = jnp.concatenate([current[1:], zeros], axis=0)
        stacked = jnp.concatenate([lower_iter, current, upper_iter], axis=1)
        product = jnp.einsum('skc,scr->skr', coarse, stacked, precision=lax.Precision.HIGHEST)
        update = solve_all(factors, (rhs - product).reshape(SUBS, N_GRP, BLK, NRHS)).reshape(SUBS, KMAX, NRHS)
        current = current + damping * update
    return current.reshape(SUBS * KMAX, NRHS)
```

```python
import functools
import jax
import jax.numpy as jnp
from jax import lax
from jax.experimental import pallas as pl
from jax.experimental.pallas import tpu as pltpu
from jax.sharding import PartitionSpec as P

SWEEPS = 6
DAMPING = 0.7
F32 = jnp.float32
BF16 = jnp.bfloat16
PLANES = 4
CX = 128
SLOTS = 512
CELLS = 512
BLK = 128
COLS = 64
GRP = 4
PANEL = 32
VMEM = pl.BlockSpec(memory_space=pltpu.VMEM)
SMEM = pl.BlockSpec(memory_space=pltpu.SMEM)


def dot(left, right):
    return jnp.dot(left, right, preferred_element_type=F32)


def dot_last(left, right):
    return lax.dot_general(left, right, (((1,), (1,)), ((), ())), preferred_element_type=F32)


def split(values):
    high = values.astype(BF16)
    low = (values - high.astype(F32)).astype(BF16)
    return high, low


def call(kernel, outs, name, scratch=(), limit=16, flops=0, nbytes=0):
    def run(*args):
        specs = [SMEM if a.dtype == jnp.int32 else VMEM for a in args]
        return pl.pallas_call(
            kernel,
            out_shape=[jax.ShapeDtypeStruct(s, d) for s, d in outs],
            in_specs=specs,
            out_specs=[VMEM] * len(outs),
            scratch_shapes=list(scratch),
            name=name,
            cost_estimate=pl.CostEstimate(flops=flops, bytes_accessed=nbytes, transcendentals=0),
            compiler_params=pltpu.CompilerParams(vmem_limit_bytes=limit << 20),
        )(*args)

    return run


def galerkin_kernel(
    info, own, right, left, across0, across1,
    eh_ref, el_ref, blocks_ref, neart_ref, fart_ref, near_ref, far_ref,
    cells, weights, images, square, field,
):
    g = info[0]
    live = info[1]
    even = info[2] == 0
    rows = lax.broadcasted_iota(jnp.int32, (CX, CX), 0)
    cols = lax.broadcasted_iota(jnp.int32, (CX, CX), 1)
    gap = jnp.abs(rows - cols)
    tri = jnp.where(gap == 0, 1.0, jnp.where(gap == 1, 0.5, 0.0)).astype(F32)
    for o in range(GRP):
        for q in range(GRP):
            dist = jnp.abs(lax.rem(g + o, GRP) - lax.rem(g + q, GRP))
            coef = jnp.where(dist == 0, 1.0, jnp.where(dist == 1, 0.5, 0.0)).astype(F32)
            weights[o * CX:(o + 1) * CX, q * CX:(q + 1) * CX] = (tri * coef).astype(BF16)
    for p in range(PLANES):
        for o in range(GRP):
            lanes = slice(p * CELLS + o * CX, p * CELLS + (o + 1) * CX)
            if o == 2:
                plane = across0[p] if p < 2 else across1[p - 2]
            else:
                plane = (own, right, None, left)[o][p]
            cells[:, lanes] = plane[:SLOTS]
            parts = plane[SLOTS:].astype(F32)
            field[p:p + 1, o * CX:(o + 1) * CX] = 16.0 + (parts[0:1] + parts[1:2] + parts[2:3])

    def slot_block(j, carry):
        row = pl.ds(pl.multiple_of(j * BLK, BLK), BLK)
        smooth = []
        for p in range(PLANES):
            smooth.append(dot(cells[row, p * CELLS:(p + 1) * CELLS], weights[...]))
        low_plane, high_plane = smooth[0].astype(BF16), smooth[PLANES - 1].astype(BF16)
        near_ref[row, :] = jnp.where(even, high_plane, low_plane)
        far_ref[row, :] = jnp.where(even, low_plane, high_plane)
        for p in range(PLANES):
            along = smooth[p]
            if p == 0:
                along = along + 0.5 * smooth[1]
            elif p == PLANES - 1:
                along = along + 0.5 * smooth[p - 1]
            else:
                along = along + 0.5 * (smooth[p - 1] + smooth[p + 1])
            own = cells[row, p * CELLS:(p + 1) * CELLS].astype(F32)
            images[:, p * CELLS:(p + 1) * CELLS] = (
                field[p:p + 1, :] * own - 2.0 * along
            ).astype(BF16)
        matrix = dot_last(images[...], cells[...])
        slot = j * BLK + lax.broadcasted_iota(jnp.int32, (BLK, SLOTS), 0)
        column = lax.broadcasted_iota(jnp.int32, (BLK, SLOTS), 1)
        matrix = matrix + jnp.where((slot == column) & (slot >= live), 1.0, 0.0).astype(F32)
        high, low = split(matrix)
        eh_ref[row, :] = high
        el_ref[row, :] = low
        square[...] = matrix
        block = square[:, pl.ds(pl.multiple_of(j * BLK, BLK), BLK)]
        blocks_ref[:, pl.ds(pl.multiple_of(j * BLK, BLK), BLK)] = 0.5 * (block + block.T)
        for c in range(GRP):
            first = (PLANES - 1) * CELLS + c * CX
            low_turned = cells[row, c * CX:(c + 1) * CX].astype(F32).T.astype(BF16)
            high_turned = cells[row, first:first + CX].astype(F32).T.astype(BF16)
            columns = pl.ds(pl.multiple_of(j * BLK, BLK), BLK)
            neart_ref[c * CX:(c + 1) * CX, columns] = jnp.where(even, high_turned, low_turned)
            fart_ref[c * CX:(c + 1) * CX, columns] = jnp.where(even, low_turned, high_turned)
        return carry

    lax.fori_loop(0, GRP, slot_block, 0)


def inverse_kernel(blocks_ref, high_ref, low_ref, work):
    work[...] = blocks_ref[...]
    lane = lax.broadcasted_iota(jnp.int32, (8, BLK), 1)
    sub = lax.broadcasted_iota(jnp.int32, (8, BLK), 0)
    base = lane - lax.rem(lane, PANEL)
    group = lax.div(lane, PANEL)
    within = lax.rem(lane, PANEL)
    group_tall = lax.div(lax.broadcasted_iota(jnp.int32, (BLK, BLK), 1), PANEL)
    count = PANEL // 8
    for p in range(BLK // PANEL):
        rows = slice(p * PANEL, (p + 1) * PANEL)
        packed = None
        for j in range(GRP):
            piece = work[rows, j * BLK:(j + 1) * BLK]
            if j != p:
                piece = pltpu.roll(piece, ((j - p) * PANEL) % BLK, 1)
            packed = piece if packed is None else jnp.where(group_tall[:PANEL] == j, piece, packed)
        tiles = [packed[8 * v:8 * v + 8] for v in range(count)]
        for k in range(0, PANEL, 2):
            v, q = k // 8, k % 8
            col0 = [jnp.take_along_axis(t, base + k, axis=1) for t in tiles]
            col1 = [jnp.take_along_axis(t, base + (k + 1), axis=1) for t in tiles]
            spread = lambda t, i: jnp.broadcast_to(t[i:i + 1], (8, BLK))
            row0, row1 = spread(tiles[v], q), spread(tiles[v], q + 1)
            p00, p10 = spread(col0[v], q), spread(col0[v], q + 1)
            p01, p11 = spread(col1[v], q), spread(col1[v], q + 1)
            scale = 1.0 / (p00 * p11 - p01 * p10)
            is0, is1 = within == k, within == k + 1
            row0 = jnp.where(is0, 1.0, jnp.where(is1, 0.0, row0))
            row1 = jnp.where(is0, 0.0, jnp.where(is1, 1.0, row1))
            new0 = (p11 * scale) * row0 - (p01 * scale) * row1
            new1 = (p00 * scale) * row1 - (p10 * scale) * row0
            for u in range(count):
                tile = jnp.where(is0 | is1, 0.0, tiles[u]) - col0[u] * new0 - col1[u] * new1
                if u == v:
                    tile = jnp.where(sub == q, new0, jnp.where(sub == q + 1, new1, tile))
                tiles[u] = tile
        packed = jnp.concatenate(tiles, axis=0)
        for j in range(GRP):
            lanes = slice(j * BLK, (j + 1) * BLK)
            block = work[:, lanes]
            pivot = pltpu.roll(packed, (-j * PANEL) % BLK, 1) if j else packed
            spot = pltpu.roll(packed, ((p - j) * PANEL) % BLK, 1) if j != p else packed
            tall = pltpu.roll(block, (-p * PANEL) % BLK, 1) if p else block
            mult = jnp.dot(
                pivot[:, :PANEL], block[rows], preferred_element_type=F32,
                precision=lax.Precision.HIGHEST,
            )
            mult = jnp.where(group_tall[:PANEL] == p, spot, mult)
            change = jnp.dot(
                tall[:, :PANEL], mult, preferred_element_type=F32,
                precision=lax.Precision.HIGHEST,
            )
            work[:, lanes] = jnp.where(group_tall == p, 0.0, block) - change
            work[rows, lanes] = mult
    high, low = split(work[...])
    high_ref[...] = high
    low_ref[...] = low


def precondition(residual, ih_ref, il_ref):
    parts = []
    for j in range(GRP):
        lanes = slice(j * BLK, (j + 1) * BLK)
        high, low = split(residual[:, lanes])
        both = dot(jnp.concatenate([high, low], axis=0), ih_ref[:, lanes])
        parts.append(both[:COLS] + both[COLS:] + dot(high, il_ref[:, lanes]))
    return DAMPING * jnp.concatenate(parts, axis=1)


def first_kernel(r_ref, ih_ref, il_ref, near_ref, far_ref, d_ref, near_out, far_out):
    delta = precondition(r_ref[...], ih_ref, il_ref)
    d_ref[...] = delta
    sent = delta.astype(BF16)
    far_out[...] = dot(sent, far_ref[...]).astype(BF16)
    near_out[...] = dot(sent, near_ref[...]).astype(BF16)


def local_kernel(r_ref, d_ref, eh_ref, el_ref, t_ref):
    high, low = split(d_ref[...])
    both = dot(jnp.concatenate([high, low], axis=0), eh_ref[...])
    t_ref[...] = r_ref[...] - (both[:COLS] + both[COLS:] + dot(high, el_ref[...]))


def sweep_kernel(
    t_ref, x_ref, far_in, near_in, neart_ref, fart_ref, ih_ref, il_ref, near_ref, far_ref,
    r_ref, d_ref, new_ref, near_out, far_out,
):
    residual = t_ref[...] + dot(near_in[...], neart_ref[...]) + dot(far_in[...], fart_ref[...])
    r_ref[...] = residual
    delta = precondition(residual, ih_ref, il_ref)
    d_ref[...] = delta
    new_ref[...] = x_ref[...] + delta
    sent = delta.astype(BF16)
    far_out[...] = dot(sent, far_ref[...]).astype(BF16)
    near_out[...] = dot(sent, near_ref[...]).astype(BF16)


def last_kernel(t_ref, x_ref, far_in, near_in, neart_ref, fart_ref, ih_ref, il_ref, out_ref):
    residual = t_ref[...] + dot(near_in[...], neart_ref[...]) + dot(far_in[...], fart_ref[...])
    out_ref[...] = x_ref[...] + precondition(residual, ih_ref, il_ref)


def shift_by(values, offset):
    return lax.ppermute(values, "grp", [(i, (i + offset) % GRP) for i in range(GRP)])


def on_device(deflation, shift_field, counts, right_sides):
    g = lax.axis_index("grp")
    subs = lax.axis_size("sub")
    live_count = counts[0]
    parity = lax.rem(lax.axis_index("sub"), 2)
    info = jnp.stack([g.astype(jnp.int32), live_count, parity.astype(jnp.int32)])
    slot_ids = lax.iota(jnp.int32, SLOTS)
    live = slot_ids < live_count
    masked = jnp.where(live[:, None, None, None], deflation, jnp.zeros((), BF16))
    planes = jnp.transpose(masked.reshape(SLOTS, PLANES, CX), (1, 0, 2))
    part0 = shift_field.astype(BF16)
    rest = shift_field - part0.astype(F32)
    part1 = rest.astype(BF16)
    part2 = (rest - part1.astype(F32)).astype(BF16)
    extra = jnp.concatenate([part0, part1, part2, jnp.zeros((PLANES, 13, CX), BF16)], axis=1)
    own = jnp.concatenate([planes, extra], axis=1)
    row_slot = g * BLK + lax.iota(jnp.int32, BLK)
    rhs = jnp.where((row_slot >= live_count)[:, None], 0.0, right_sides).T
    left = shift_by(own, 1)
    right = shift_by(own, -1)
    start = lax.all_to_all(rhs, "grp", 0, 1, tiled=True)
    across0 = shift_by(left[:2], 1)
    across1 = shift_by(right[2:], -1)

    square = (SLOTS, SLOTS)
    eh, el, blocks, neart, fart, near, far = call(
        galerkin_kernel,
        [(square, BF16), (square, BF16), ((BLK, SLOTS), F32)] + [(square, BF16)] * 4,
        "galerkin",
        scratch=[
            pltpu.VMEM((SLOTS, PLANES * CELLS), BF16),
            pltpu.VMEM((CELLS, CELLS), BF16),
            pltpu.VMEM((BLK, PLANES * CELLS), BF16),
            pltpu.VMEM((BLK, SLOTS), F32),
            pltpu.VMEM((8, CELLS), F32),
        ],
        limit=24,
        flops=2 * 10**9,
        nbytes=6 << 20,
    )(info, own, right, left, across0, across1)
    ih, il = call(
        inverse_kernel,
        [((BLK, SLOTS), BF16)] * 2,
        "inverse",
        scratch=[pltpu.VMEM((BLK, SLOTS), F32)],
        flops=10**9,
        nbytes=1 << 19,
    )(blocks)

    vec = (COLS, SLOTS)
    r = start
    d, near_msg, far_msg = call(
        first_kernel, [(vec, F32), (vec, BF16), (vec, BF16)], "first",
        flops=10**8, nbytes=2 << 20,
    )(r, ih, il, near, far)
    x = d
    near_pairs = [(i, i ^ 1) for i in range(subs)]
    far_pairs = [(i, ((i + 1) ^ 1) - 1) for i in range(1, subs - 1)]
    for sweep in range(1, SWEEPS):
        far_got = lax.ppermute(far_msg, "sub", far_pairs)
        near_got = lax.ppermute(near_msg, "sub", near_pairs)
        (t,) = call(local_kernel, [(vec, F32)], "local", flops=10**8, nbytes=1 << 20)(r, d, eh, el)
        if sweep < SWEEPS - 1:
            r, d, x, near_msg, far_msg = call(
                sweep_kernel,
                [(vec, F32), (vec, F32), (vec, F32), (vec, BF16), (vec, BF16)],
                "sweep", flops=2 * 10**8, nbytes=3 << 20,
            )(t, x, far_got, near_got, neart, fart, ih, il, near, far)
        else:
            (x,) = call(
                last_kernel, [(vec, F32)], "last", flops=10**8, nbytes=2 << 20,
            )(t, x, far_got, near_got, neart, fart, ih, il)
    return lax.all_to_all(x, "grp", 1, 0, tiled=True).T


def solution(mesh):
    in_specs = (
        P(None, "sub", "grp", None),
        P("sub", "grp", None),
        P("sub"),
        P(("sub", "grp"), None),
    )
    return jax.shard_map(
        on_device, mesh=mesh, in_specs=in_specs,
        out_specs=P(("sub", "grp"), None), check_vma=False,
    )
```

```python
import jax
import jax.numpy as jnp
from jax import lax
from jax.experimental import pallas as pl
from jax.experimental.pallas import tpu as pltpu
from jax.sharding import PartitionSpec as P

SWEEPS = 6
DAMPING = 0.7
F32 = jnp.float32
BF16 = jnp.bfloat16
PLANES = 4
CX = 128
SLOTS = 512
HALF = 256
CELLS = 512
BLK = 128
COLS = 64
GRP = 4
PANEL = 32
VMEM = pl.BlockSpec(memory_space=pltpu.VMEM)
SMEM = pl.BlockSpec(memory_space=pltpu.SMEM)


def dot(left, right):
    return jnp.dot(left, right, preferred_element_type=F32)


def dot_last(left, right):
    return lax.dot_general(left, right, (((1,), (1,)), ((), ())), preferred_element_type=F32)


def split(values):
    high = values.astype(BF16)
    low = (values - high.astype(F32)).astype(BF16)
    return high, low


def call(kernel, outs, scratch=(), limit=16, flops=0, nbytes=0):
    def run(*args):
        specs = [SMEM if a.dtype == jnp.int32 else VMEM for a in args]
        return pl.pallas_call(
            kernel,
            out_shape=[jax.ShapeDtypeStruct(s, d) for s, d in outs],
            in_specs=specs,
            out_specs=[VMEM] * len(outs),
            scratch_shapes=list(scratch),
            cost_estimate=pl.CostEstimate(flops=flops, bytes_accessed=nbytes, transcendentals=0),
            compiler_params=pltpu.CompilerParams(vmem_limit_bytes=limit << 20),
        )(*args)

    return run


def images_kernel(
    info, own0, own1, right0, right1, across0, across1, left0, left1, got,
    cells, images, blocks_ref, neart_ref, fart_ref, near_ref, far_ref,
    weights, field,
):
    g = info[0]
    live = info[1]
    even = info[2] == 0
    parts = ((own0, own1), (right0, right1), (across0, across1), (left0, left1))
    rows = lax.broadcasted_iota(jnp.int32, (CX, CX), 0)
    cols = lax.broadcasted_iota(jnp.int32, (CX, CX), 1)
    gap = jnp.abs(rows - cols)
    tri = jnp.where(gap == 0, 1.0, jnp.where(gap == 1, 0.5, 0.0)).astype(F32)
    for o in range(GRP):
        for q in range(GRP):
            dist = jnp.abs(lax.rem(g + o, GRP) - lax.rem(g + q, GRP))
            coef = jnp.where(dist == 0, 1.0, jnp.where(dist == 1, 0.5, 0.0)).astype(F32)
            weights[o * CX:(o + 1) * CX, q * CX:(q + 1) * CX] = (tri * coef).astype(BF16)
    for p in range(PLANES):
        for o in range(GRP):
            plane = parts[o][p // 2][p % 2]
            cells[:, p * CELLS + o * CX:p * CELLS + (o + 1) * CX] = plane[...]
    for o in range(GRP):
        field[:, o * CX:(o + 1) * CX] = 16.0 + got[lax.rem(g + o, GRP), COLS:, :]

    def slot_half(h, carry):
        row = pl.ds(pl.multiple_of(h * HALF, HALF), HALF)
        smooth = []
        for p in range(PLANES):
            smooth.append(dot(cells[row, p * CELLS:(p + 1) * CELLS], weights[...]))
        low_plane, high_plane = smooth[0].astype(BF16), smooth[PLANES - 1].astype(BF16)
        near_ref[row, :] = jnp.where(even, high_plane, low_plane)
        far_ref[row, :] = jnp.where(even, low_plane, high_plane)
        for p in range(PLANES):
            along = smooth[p]
            if p == 0:
                along = along + 0.5 * smooth[1]
            elif p == PLANES - 1:
                along = along + 0.5 * smooth[p - 1]
            else:
                along = along + 0.5 * (smooth[p - 1] + smooth[p + 1])
            own = cells[row, p * CELLS:(p + 1) * CELLS].astype(F32)
            images[row, p * CELLS:(p + 1) * CELLS] = (
                field[p:p + 1, :] * own - 2.0 * along
            ).astype(BF16)
        for i in range(HALF // BLK):
            first_slot = pl.multiple_of(h * HALF + i * BLK, BLK)
            line = pl.ds(first_slot, BLK)
            block = dot_last(images[line, :], cells[line, :])
            pad = (gap == 0) & (first_slot + rows >= live)
            blocks_ref[:, line] = 0.5 * (block + block.T) + jnp.where(pad, 1.0, 0.0).astype(F32)
        for c in range(GRP):
            first = (PLANES - 1) * CELLS + c * CX
            low_turned = cells[row, c * CX:(c + 1) * CX].astype(F32).T.astype(BF16)
            high_turned = cells[row, first:first + CX].astype(F32).T.astype(BF16)
            neart_ref[c * CX:(c + 1) * CX, row] = jnp.where(even, high_turned, low_turned)
            fart_ref[c * CX:(c + 1) * CX, row] = jnp.where(even, low_turned, high_turned)
        return carry

    lax.fori_loop(0, SLOTS // HALF, slot_half, 0)


def matrix_kernel(info, cells, images, r_ref, d_ref, eh_ref, el_ref, t_ref):
    live = info[1]

    def slot_half(h, carry):
        row = pl.ds(pl.multiple_of(h * HALF, HALF), HALF)
        matrix = dot_last(images[row, :], cells[...])
        slot = h * HALF + lax.broadcasted_iota(jnp.int32, (HALF, SLOTS), 0)
        column = lax.broadcasted_iota(jnp.int32, (HALF, SLOTS), 1)
        matrix = matrix + jnp.where((slot == column) & (slot >= live), 1.0, 0.0).astype(F32)
        high, low = split(matrix)
        eh_ref[row, :] = high
        el_ref[row, :] = low
        return carry

    lax.fori_loop(0, SLOTS // HALF, slot_half, 0)
    local_kernel(r_ref, d_ref, eh_ref, el_ref, t_ref)


def invert2(m):
    scale = 1.0 / (m[0] * m[3] - m[1] * m[2])
    return m[3] * scale, -(m[1] * scale), -(m[2] * scale), m[0] * scale


def times2(m, n):
    return (
        m[0] * n[0] + m[1] * n[2], m[0] * n[1] + m[1] * n[3],
        m[2] * n[0] + m[3] * n[2], m[2] * n[1] + m[3] * n[3],
    )


def invert4(m):
    a = (m[0][0], m[0][1], m[1][0], m[1][1])
    b = (m[0][2], m[0][3], m[1][2], m[1][3])
    c = (m[2][0], m[2][1], m[3][0], m[3][1])
    d = (m[2][2], m[2][3], m[3][2], m[3][3])
    ai = invert2(a)
    aib, cai = times2(ai, b), times2(c, ai)
    si = invert2(tuple(u - v for u, v in zip(d, times2(c, aib))))
    x, y = times2(aib, si), times2(si, cai)
    z = tuple(u + v for u, v in zip(ai, times2(x, cai)))
    return (
        (z[0], z[1], -x[0], -x[1]), (z[2], z[3], -x[2], -x[3]),
        (-y[0], -y[1], si[0], si[1]), (-y[2], -y[3], si[2], si[3]),
    )


def inverse_kernel(blocks_ref, high_ref, low_ref, work):
    work[...] = blocks_ref[...]
    lane = lax.broadcasted_iota(jnp.int32, (8, BLK), 1)
    sub = lax.broadcasted_iota(jnp.int32, (8, BLK), 0)
    base = lane - lax.rem(lane, PANEL)
    within = lax.rem(lane, PANEL)
    group = lax.div(lax.broadcasted_iota(jnp.int32, (PANEL, BLK), 1), PANEL)
    count = PANEL // 8
    panels = BLK // PANEL
    spread = lambda t, i: jnp.broadcast_to(t[i:i + 1], (8, BLK))
    turn = lambda t, n: pltpu.roll(t, (n * PANEL) % BLK, 1) if n % panels else t
    wide = lambda m, n: jnp.dot(m, n, preferred_element_type=F32, precision=lax.Precision.HIGHEST)
    for p in range(panels):
        rows = slice(p * PANEL, (p + 1) * PANEL)
        packed = None
        for j in range(GRP):
            piece = turn(work[rows, j * BLK:(j + 1) * BLK], j - p)
            packed = piece if packed is None else jnp.where(group == j, piece, packed)
        tiles = [packed[8 * v:8 * v + 8] for v in range(count)]
        for k in range(0, PANEL, 4):
            v, q = k // 8, k % 8
            cols = [[jnp.take_along_axis(t, base + (k + c), axis=1) for t in tiles] for c in range(4)]
            pivot = invert4([[spread(cols[c][v], q + i) for c in range(4)] for i in range(4)])
            inside = (within >= k) & (within < k + 4)
            lines = [
                jnp.where(inside, jnp.where(within == k + i, 1.0, 0.0), spread(tiles[v], q + i))
                for i in range(4)
            ]
            new = [
                (pivot[i][0] * lines[0] + pivot[i][1] * lines[1])
                + (pivot[i][2] * lines[2] + pivot[i][3] * lines[3])
                for i in range(4)
            ]
            for u in range(count):
                tile = jnp.where(inside, 0.0, tiles[u]) - (
                    (cols[0][u] * new[0] + cols[1][u] * new[1])
                    + (cols[2][u] * new[2] + cols[3][u] * new[3])
                )
                if u == v:
                    for i in range(4):
                        tile = jnp.where(sub == q + i, new[i], tile)
                tiles[u] = tile
        packed = jnp.concatenate(tiles, axis=0)
        mults = []
        for j in range(GRP):
            mult = wide(turn(packed, -j)[:, :PANEL], work[rows, j * BLK:(j + 1) * BLK])
            mults.append(jnp.where(group == p, turn(packed, p - j), mult))
        for step in range(1, panels):
            other = (p + step) % panels
            others = slice(other * PANEL, (other + 1) * PANEL)
            for j in range(GRP):
                lanes = slice(j * BLK, (j + 1) * BLK)
                block = work[others, lanes]
                change = wide(turn(block, -p)[:, :PANEL], mults[j])
                work[others, lanes] = jnp.where(group == p, 0.0, block) - change
        for j in range(GRP):
            work[rows, j * BLK:(j + 1) * BLK] = mults[j]
    high, low = split(work[...])
    high_ref[...] = high
    low_ref[...] = low


def precondition(residual, ih_ref, il_ref):
    parts = []
    for j in range(GRP):
        lanes = slice(j * BLK, (j + 1) * BLK)
        high, low = split(residual[:, lanes])
        both = dot(jnp.concatenate([high, low], axis=0), ih_ref[:, lanes])
        parts.append(both[:COLS] + both[COLS:] + dot(high, il_ref[:, lanes]))
    return DAMPING * jnp.concatenate(parts, axis=1)


def send(delta, near_ref, far_ref, near_out, far_out):
    sent = delta.astype(BF16)
    far_out[...] = dot(sent, far_ref[...]).astype(BF16)
    near_out[...] = dot(sent, near_ref[...]).astype(BF16)


def first_kernel(got, ih_ref, il_ref, near_ref, far_ref, r_ref, d_ref, near_out, far_out):
    for j in range(GRP):
        r_ref[:, j * BLK:(j + 1) * BLK] = got[j, :COLS, :]
    delta = precondition(r_ref[...], ih_ref, il_ref)
    d_ref[...] = delta
    send(delta, near_ref, far_ref, near_out, far_out)


def local_kernel(r_ref, d_ref, eh_ref, el_ref, t_ref):
    high, low = split(d_ref[...])
    both = dot(jnp.concatenate([high, low], axis=0), eh_ref[...])
    t_ref[...] = r_ref[...] - (both[:COLS] + both[COLS:] + dot(high, el_ref[...]))


def sweep_kernel(
    t_ref, far_in, near_in, neart_ref, fart_ref, ih_ref, il_ref, near_ref, far_ref,
    r_ref, d_ref, near_out, far_out,
):
    residual = t_ref[...] + dot(near_in[...], neart_ref[...]) + dot(far_in[...], fart_ref[...])
    r_ref[...] = residual
    delta = precondition(residual, ih_ref, il_ref)
    d_ref[...] = delta
    send(delta, near_ref, far_ref, near_out, far_out)


def both_kernel(r_ref, d_ref, x_ref, eh_ref, el_ref, t_ref, new_ref):
    new_ref[...] = x_ref[...] + d_ref[...]
    local_kernel(r_ref, d_ref, eh_ref, el_ref, t_ref)


def last_kernel(t_ref, x_ref, far_in, near_in, neart_ref, fart_ref, ih_ref, il_ref, out_ref):
    residual = t_ref[...] + dot(near_in[...], neart_ref[...]) + dot(far_in[...], fart_ref[...])
    out_ref[...] = x_ref[...] + precondition(residual, ih_ref, il_ref)


def shift_by(values, offset):
    return lax.ppermute(values, "grp", [(i, (i + offset) % GRP) for i in range(GRP)])


def on_device_steps(deflation, shift_field, counts, right_sides):
    g = lax.axis_index("grp")
    subs = lax.axis_size("sub")
    live_count = counts[0]
    parity = lax.rem(lax.axis_index("sub"), 2)
    info = jnp.stack([g.astype(jnp.int32), live_count, parity.astype(jnp.int32)])
    slot_ids = lax.iota(jnp.int32, SLOTS)
    live = slot_ids < live_count
    masked = jnp.where(live[:, None, None, None], deflation, jnp.zeros((), BF16))
    planes = jnp.transpose(masked.reshape(SLOTS, PLANES, CX), (1, 0, 2))
    own0, own1 = planes[:2], planes[2:]
    row_slot = g * BLK + lax.iota(jnp.int32, BLK)
    rhs = jnp.where((row_slot >= live_count)[:, None], 0.0, right_sides).T.reshape(GRP, COLS, BLK)
    field = jnp.zeros((8, CX), F32).at[:PLANES].set(shift_field.reshape(PLANES, CX))
    pieces = jnp.concatenate([rhs, jnp.broadcast_to(field, (GRP, 8, CX))], axis=1)
    left0 = shift_by(own0, 1)
    right1 = shift_by(own1, -1)
    left1 = shift_by(own1, 1)
    right0 = shift_by(own0, -1)
    across0 = shift_by(left0, 1)
    across1 = shift_by(right1, -1)
    got = lax.all_to_all(pieces, "grp", 0, 0)

    square = (SLOTS, SLOTS)
    tall = (SLOTS, PLANES * CELLS)
    cells, images, blocks, neart, fart, near, far = call(
        images_kernel,
        [(tall, BF16), (tall, BF16), ((BLK, SLOTS), F32)] + [(square, BF16)] * 4,
        scratch=[pltpu.VMEM((CELLS, CELLS), BF16), pltpu.VMEM((8, CELLS), F32)],
        limit=24,
        flops=2 * 10**9,
        nbytes=8 << 20,
    )(info, own0, own1, right0, right1, across0, across1, left0, left1, got)
    ih, il = call(
        inverse_kernel,
        [((BLK, SLOTS), BF16)] * 2,
        scratch=[pltpu.VMEM((BLK, SLOTS), F32)],
        flops=10**9,
        nbytes=1 << 19,
    )(blocks)

    vec = (COLS, SLOTS)
    r, d, near_msg, far_msg = call(
        first_kernel, [(vec, F32), (vec, F32), (vec, BF16), (vec, BF16)],
        flops=10**8, nbytes=1 << 20,
    )(got, ih, il, near, far)
    x = d
    near_pairs = [(i, i ^ 1) for i in range(subs)]
    far_pairs = [(i, ((i + 1) ^ 1) - 1) for i in range(1, subs - 1)]
    for sweep in range(1, SWEEPS):
        far_got = lax.ppermute(far_msg, "sub", far_pairs)
        near_got = lax.ppermute(near_msg, "sub", near_pairs)
        if sweep == 1:
            eh, el, t = call(
                matrix_kernel, [(square, BF16), (square, BF16), (vec, F32)],
                limit=16, flops=10**9, nbytes=5 << 20,
            )(info, cells, images, r, d)
        else:
            t, x = call(
                both_kernel, [(vec, F32), (vec, F32)], flops=10**8, nbytes=1 << 20,
            )(r, d, x, eh, el)
        if sweep < SWEEPS - 1:
            r, d, near_msg, far_msg = call(
                sweep_kernel, [(vec, F32), (vec, F32), (vec, BF16), (vec, BF16)],
                flops=2 * 10**8, nbytes=3 << 20,
            )(t, far_got, near_got, neart, fart, ih, il, near, far)
        else:
            (x,) = call(
                last_kernel, [(vec, F32)], flops=10**8, nbytes=2 << 20,
            )(t, x, far_got, near_got, neart, fart, ih, il)
    return lax.all_to_all(x, "grp", 1, 0, tiled=True).T


def solution(mesh):
    in_specs = (
        P(None, "sub", "grp", None),
        P("sub", "grp", None),
        P("sub"),
        P(("sub", "grp"), None),
    )
    return jax.shard_map(
        on_device_steps, mesh=mesh, in_specs=in_specs,
        out_specs=P(("sub", "grp"), None), check_vma=False,
    )
```

```python
import jax
import jax.numpy as jnp
from jax import lax
from jax.experimental import pallas as pl
from jax.experimental.pallas import tpu as pltpu
from jax.sharding import PartitionSpec as P

SWEEPS = 6
DAMPING = 0.7
F32 = jnp.float32
BF16 = jnp.bfloat16
PLANES = 4
CX = 128
SLOTS = 512
HALF = 256
CELLS = 512
BLK = 128
COLS = 64
GRP = 4
PANEL = 32
VMEM = pl.BlockSpec(memory_space=pltpu.VMEM)
SMEM = pl.BlockSpec(memory_space=pltpu.SMEM)


def dot(left, right):
    return jnp.dot(left, right, preferred_element_type=F32)


def dot_last(left, right):
    return lax.dot_general(left, right, (((1,), (1,)), ((), ())), preferred_element_type=F32)


def split(values):
    high = values.astype(BF16)
    low = (values - high.astype(F32)).astype(BF16)
    return high, low


def call(kernel, outs, scratch=(), limit=16, flops=0, nbytes=0):
    def run(*args):
        specs = [SMEM if a.dtype == jnp.int32 else VMEM for a in args]
        return pl.pallas_call(
            kernel,
            out_shape=[jax.ShapeDtypeStruct(s, d) for s, d in outs],
            in_specs=specs,
            out_specs=[VMEM] * len(outs),
            scratch_shapes=list(scratch),
            cost_estimate=pl.CostEstimate(flops=flops, bytes_accessed=nbytes, transcendentals=0),
            compiler_params=pltpu.CompilerParams(vmem_limit_bytes=limit << 20),
        )(*args)

    return run


def owners(g):
    even = lax.rem(g, 2) == 0
    other = jnp.where(even, g + 1, g - 1)
    return g, other, lax.rem(g + 2, GRP), GRP - 1 - g


def images_kernel(
    info, own0, own1, side0, side1, across0, across1, back0, back1, got,
    cells, images, blocks_ref, neart_ref, fart_ref, near_ref, far_ref,
    weights, field,
):
    g = info[0]
    live = info[1]
    even = info[2] == 0
    parts = ((own0, own1), (side0, side1), (across0, across1), (back0, back1))
    row_of = owners(g)
    rows = lax.broadcasted_iota(jnp.int32, (CX, CX), 0)
    cols = lax.broadcasted_iota(jnp.int32, (CX, CX), 1)
    gap = jnp.abs(rows - cols)
    slots = lax.broadcasted_iota(jnp.int32, (SLOTS, CX), 0)
    tri = jnp.where(gap == 0, 1.0, jnp.where(gap == 1, 0.5, 0.0)).astype(F32)
    none = jnp.zeros((CX, CX), BF16)
    weights[...] = jnp.concatenate(
        [
            jnp.concatenate([tri.astype(BF16), none], axis=1),
            jnp.concatenate([none, tri.astype(BF16)], axis=1),
        ],
        axis=0,
    )
    outer = jnp.where((g == 1) | (g == 2), 0.5, 0.0).astype(F32)
    inner = 0.5 - outer
    for p in range(PLANES):
        for o in range(GRP):
            plane = parts[o][p // 2][p % 2]
            cells[:, p * CELLS + o * CX:p * CELLS + (o + 1) * CX] = jnp.where(
                slots < live, plane[...].astype(F32), 0.0
            ).astype(BF16)
    for o in range(GRP):
        field[:, o * CX:(o + 1) * CX] = 16.0 + got[row_of[o], COLS:, :]

    def slot_half(h, carry):
        row = slice(h * HALF, (h + 1) * HALF)
        smooth = []
        for p in range(PLANES):
            low_pair = dot(cells[row, p * CELLS:p * CELLS + 2 * CX], weights[...])
            high_pair = dot(cells[row, p * CELLS + 2 * CX:(p + 1) * CELLS], weights[...])
            s0, s1 = low_pair[:, :CX], low_pair[:, CX:]
            s2, s3 = high_pair[:, :CX], high_pair[:, CX:]
            smooth.append(
                jnp.concatenate(
                    [
                        s0 + 0.5 * s1 + outer * s3,
                        s1 + 0.5 * s0 + inner * s2,
                        s2 + 0.5 * s3 + inner * s1,
                        s3 + 0.5 * s2 + outer * s0,
                    ],
                    axis=1,
                )
            )
        low_plane, high_plane = smooth[0].astype(BF16), smooth[PLANES - 1].astype(BF16)
        near_ref[row, :] = jnp.where(even, high_plane, low_plane)
        far_ref[row, :] = jnp.where(even, low_plane, high_plane)
        for p in range(PLANES):
            along = smooth[p]
            if p == 0:
                along = along + 0.5 * smooth[1]
            elif p == PLANES - 1:
                along = along + 0.5 * smooth[p - 1]
            else:
                along = along + 0.5 * (smooth[p - 1] + smooth[p + 1])
            own = cells[row, p * CELLS:(p + 1) * CELLS].astype(F32)
            images[row, p * CELLS:(p + 1) * CELLS] = (
                field[p:p + 1, :] * own - 2.0 * along
            ).astype(BF16)
        for i in range(HALF // BLK):
            first_slot = h * HALF + i * BLK
            line = slice(first_slot, first_slot + BLK)
            block = dot_last(images[line, :], cells[line, :])
            pad = (gap == 0) & (first_slot + rows >= live)
            blocks_ref[:, line] = 0.5 * (block + block.T) + jnp.where(pad, 1.0, 0.0).astype(F32)
        for c in range(GRP):
            first = (PLANES - 1) * CELLS + c * CX
            low_turned = cells[row, c * CX:(c + 1) * CX].astype(F32).T.astype(BF16)
            high_turned = cells[row, first:first + CX].astype(F32).T.astype(BF16)
            neart_ref[c * CX:(c + 1) * CX, row] = jnp.where(even, high_turned, low_turned)
            fart_ref[c * CX:(c + 1) * CX, row] = jnp.where(even, low_turned, high_turned)
        return carry

    for h in range(SLOTS // HALF):
        slot_half(h, 0)


def invert2(m):
    scale = 1.0 / (m[0] * m[3] - m[1] * m[2])
    return m[3] * scale, -(m[1] * scale), -(m[2] * scale), m[0] * scale


def times2(m, n):
    return (
        m[0] * n[0] + m[1] * n[2], m[0] * n[1] + m[1] * n[3],
        m[2] * n[0] + m[3] * n[2], m[2] * n[1] + m[3] * n[3],
    )


def invert4(m):
    a = (m[0][0], m[0][1], m[1][0], m[1][1])
    b = (m[0][2], m[0][3], m[1][2], m[1][3])
    c = (m[2][0], m[2][1], m[3][0], m[3][1])
    d = (m[2][2], m[2][3], m[3][2], m[3][3])
    ai = invert2(a)
    aib, cai = times2(ai, b), times2(c, ai)
    si = invert2(tuple(u - v for u, v in zip(d, times2(c, aib))))
    x, y = times2(aib, si), times2(si, cai)
    z = tuple(u + v for u, v in zip(ai, times2(x, cai)))
    return (
        (z[0], z[1], -x[0], -x[1]), (z[2], z[3], -x[2], -x[3]),
        (-y[0], -y[1], si[0], si[1]), (-y[2], -y[3], si[2], si[3]),
    )


def inverse_kernel(info, blocks_ref, cells, images, high_ref, low_ref, eh_ref, el_ref, work):
    live = info[1]
    work[...] = blocks_ref[...]
    lane = lax.broadcasted_iota(jnp.int32, (8, BLK), 1)
    sub = lax.broadcasted_iota(jnp.int32, (8, BLK), 0)
    base = lane - lax.rem(lane, PANEL)
    within = lax.rem(lane, PANEL)
    group = lax.div(lax.broadcasted_iota(jnp.int32, (PANEL, BLK), 1), PANEL)
    count = PANEL // 8
    panels = BLK // PANEL
    spread = lambda t, i: jnp.broadcast_to(t[i:i + 1], (8, BLK))
    turn = lambda t, n: pltpu.roll(t, (n * PANEL) % BLK, 1) if n % panels else t
    wide = lambda m, n: jnp.dot(m, n, preferred_element_type=F32, precision=lax.Precision.HIGHEST)
    for p in range(panels):
        rows = slice(p * PANEL, (p + 1) * PANEL)
        packed = None
        for j in range(GRP):
            piece = turn(work[rows, j * BLK:(j + 1) * BLK], j - p)
            packed = piece if packed is None else jnp.where(group == j, piece, packed)
        tiles = [packed[8 * v:8 * v + 8] for v in range(count)]
        lines = slice(p // 2 * HALF, (p // 2 + 1) * HALF)
        columns = slice(p % 2 * HALF, (p % 2 + 1) * HALF)
        matrix = dot_last(images[lines, :], cells[columns, :])
        if p // 2 == p % 2:
            slot = lax.broadcasted_iota(jnp.int32, (HALF, HALF), 0)
            column = lax.broadcasted_iota(jnp.int32, (HALF, HALF), 1)
            pad = (slot == column) & (slot + p // 2 * HALF >= live)
            matrix = matrix + jnp.where(pad, 1.0, 0.0).astype(F32)
        matrix_high, matrix_low = split(matrix)
        eh_ref[lines, columns] = matrix_high
        el_ref[lines, columns] = matrix_low
        for k in range(0, PANEL, 4):
            v, q = k // 8, k % 8
            cols = [[jnp.take_along_axis(t, base + (k + c), axis=1) for t in tiles] for c in range(4)]
            pivot = invert4([[spread(cols[c][v], q + i) for c in range(4)] for i in range(4)])
            inside = (within >= k) & (within < k + 4)
            pivot_rows = [
                jnp.where(inside, jnp.where(within == k + i, 1.0, 0.0), spread(tiles[v], q + i))
                for i in range(4)
            ]
            new = [
                (pivot[i][0] * pivot_rows[0] + pivot[i][1] * pivot_rows[1])
                + (pivot[i][2] * pivot_rows[2] + pivot[i][3] * pivot_rows[3])
                for i in range(4)
            ]
            for u in range(count):
                tile = jnp.where(inside, 0.0, tiles[u]) - (
                    (cols[0][u] * new[0] + cols[1][u] * new[1])
                    + (cols[2][u] * new[2] + cols[3][u] * new[3])
                )
                if u == v:
                    for i in range(4):
                        tile = jnp.where(sub == q + i, new[i], tile)
                tiles[u] = tile
        packed = jnp.concatenate(tiles, axis=0)
        mults = []
        for j in range(GRP):
            mult = wide(turn(packed, -j)[:, :PANEL], work[rows, j * BLK:(j + 1) * BLK])
            mults.append(jnp.where(group == p, turn(packed, p - j), mult))
        for step in range(1, panels):
            other = (p + step) % panels
            others = slice(other * PANEL, (other + 1) * PANEL)
            for j in range(GRP):
                lanes = slice(j * BLK, (j + 1) * BLK)
                block = work[others, lanes]
                change = wide(turn(block, -p)[:, :PANEL], mults[j])
                work[others, lanes] = jnp.where(group == p, 0.0, block) - change
        for j in range(GRP):
            work[rows, j * BLK:(j + 1) * BLK] = mults[j]
    high, low = split(work[...])
    high_ref[...] = high
    low_ref[...] = low


def precondition(residual, ih_ref, il_ref):
    parts = []
    for j in range(GRP):
        lanes = slice(j * BLK, (j + 1) * BLK)
        high, low = split(residual[:, lanes])
        both = dot(jnp.concatenate([high, low], axis=0), ih_ref[:, lanes])
        parts.append(both[:COLS] + both[COLS:] + dot(high, il_ref[:, lanes]))
    return DAMPING * jnp.concatenate(parts, axis=1)


def send(delta, near_ref, far_ref, near_out, far_out):
    sent = delta.astype(BF16)
    far_out[...] = dot(sent, far_ref[...]).astype(BF16)
    near_out[...] = dot(sent, near_ref[...]).astype(BF16)


def first_kernel(got, ih_ref, il_ref, near_ref, far_ref, r_ref, d_ref, near_out, far_out):
    for j in range(GRP):
        r_ref[:, j * BLK:(j + 1) * BLK] = got[j, :COLS, :]
    delta = precondition(r_ref[...], ih_ref, il_ref)
    d_ref[...] = delta
    send(delta, near_ref, far_ref, near_out, far_out)


def local_kernel(r_ref, d_ref, eh_ref, el_ref, t_ref):
    high, low = split(d_ref[...])
    both = dot(jnp.concatenate([high, low], axis=0), eh_ref[...])
    t_ref[...] = r_ref[...] - (both[:COLS] + both[COLS:] + dot(high, el_ref[...]))


def sweep_kernel(
    t_ref, far_in, near_in, neart_ref, fart_ref, ih_ref, il_ref, near_ref, far_ref,
    r_ref, d_ref, near_out, far_out,
):
    residual = t_ref[...] + dot(near_in[...], neart_ref[...]) + dot(far_in[...], fart_ref[...])
    r_ref[...] = residual
    delta = precondition(residual, ih_ref, il_ref)
    d_ref[...] = delta
    send(delta, near_ref, far_ref, near_out, far_out)


def both_kernel(r_ref, d_ref, x_ref, eh_ref, el_ref, t_ref, new_ref):
    new_ref[...] = x_ref[...] + d_ref[...]
    local_kernel(r_ref, d_ref, eh_ref, el_ref, t_ref)


def last_kernel(t_ref, x_ref, far_in, near_in, neart_ref, fart_ref, ih_ref, il_ref, out_ref):
    residual = t_ref[...] + dot(near_in[...], neart_ref[...]) + dot(far_in[...], fart_ref[...])
    out_ref[...] = x_ref[...] + precondition(residual, ih_ref, il_ref)


SIDE = ((0, 1), (1, 0), (2, 3), (3, 2))
BACK = ((0, 3), (3, 0), (1, 2), (2, 1))


def swap(values, pairs):
    return lax.ppermute(values, "grp", pairs)


def on_device_steps(deflation, shift_field, counts, right_sides):
    g = lax.axis_index("grp")
    subs = lax.axis_size("sub")
    live_count = counts[0]
    parity = lax.rem(lax.axis_index("sub"), 2)
    info = jnp.stack([g.astype(jnp.int32), live_count, parity.astype(jnp.int32)])
    planes = jnp.transpose(deflation.reshape(SLOTS, PLANES, CX), (1, 0, 2))
    own0, own1 = planes[:2], planes[2:]
    row_slot = g * BLK + lax.iota(jnp.int32, BLK)
    rhs = jnp.where((row_slot >= live_count)[:, None], 0.0, right_sides).T.reshape(GRP, COLS, BLK)
    field = jnp.zeros((8, CX), F32).at[:PLANES].set(shift_field.reshape(PLANES, CX))
    pieces = jnp.concatenate([rhs, jnp.broadcast_to(field, (GRP, 8, CX))], axis=1)
    side0 = swap(own0, SIDE)
    back1 = swap(own1, BACK)
    back0 = swap(own0, BACK)
    side1 = swap(own1, SIDE)
    across0 = swap(side0, BACK)
    across1 = swap(back1, SIDE)
    got = lax.all_to_all(pieces, "grp", 0, 0)

    square = (SLOTS, SLOTS)
    tall = (SLOTS, PLANES * CELLS)
    cells, images, blocks, neart, fart, near, far = call(
        images_kernel,
        [(tall, BF16), (tall, BF16), ((BLK, SLOTS), F32)] + [(square, BF16)] * 4,
        scratch=[pltpu.VMEM((2 * CX, 2 * CX), BF16), pltpu.VMEM((8, CELLS), F32)],
        limit=24,
        flops=2 * 10**9,
        nbytes=8 << 20,
    )(info, own0, own1, side0, side1, across0, across1, back0, back1, got)
    ih, il, eh, el = call(
        inverse_kernel,
        [((BLK, SLOTS), BF16)] * 2 + [(square, BF16)] * 2,
        scratch=[pltpu.VMEM((BLK, SLOTS), F32)],
        flops=10**9,
        nbytes=5 << 20,
    )(info, blocks, cells, images)

    vec = (COLS, SLOTS)
    r, d, near_msg, far_msg = call(
        first_kernel, [(vec, F32), (vec, F32), (vec, BF16), (vec, BF16)],
        flops=10**8, nbytes=1 << 20,
    )(got, ih, il, near, far)
    x = d
    near_pairs = [(i, i ^ 1) for i in range(subs)]
    far_pairs = [(i, ((i + 1) ^ 1) - 1) for i in range(1, subs - 1)]
    for sweep in range(1, SWEEPS):
        far_got = lax.ppermute(far_msg, "sub", far_pairs)
        near_got = lax.ppermute(near_msg, "sub", near_pairs)
        if sweep == 1:
            (t,) = call(local_kernel, [(vec, F32)], flops=10**8, nbytes=1 << 20)(r, d, eh, el)
        else:
            t, x = call(
                both_kernel, [(vec, F32), (vec, F32)], flops=10**8, nbytes=1 << 20,
            )(r, d, x, eh, el)
        if sweep < SWEEPS - 1:
            r, d, near_msg, far_msg = call(
                sweep_kernel, [(vec, F32), (vec, F32), (vec, BF16), (vec, BF16)],
                flops=2 * 10**8, nbytes=3 << 20,
            )(t, far_got, near_got, neart, fart, ih, il, near, far)
        else:
            (x,) = call(
                last_kernel, [(vec, F32)], flops=10**8, nbytes=2 << 20,
            )(t, x, far_got, near_got, neart, fart, ih, il)
    return lax.all_to_all(x, "grp", 1, 0, tiled=True).T


def solution(mesh):
    in_specs = (
        P(None, "sub", "grp", None),
        P("sub", "grp", None),
        P("sub"),
        P(("sub", "grp"), None),
    )
    return jax.shard_map(
        on_device_steps, mesh=mesh, in_specs=in_specs,
        out_specs=P(("sub", "grp"), None), check_vma=False,
    )
```

```python
import jax
import jax.numpy as jnp
from jax import lax
from jax.experimental import pallas as pl
from jax.experimental.pallas import tpu as pltpu
from jax.sharding import PartitionSpec as P

SWEEPS = 6
DAMPING = 0.7
F32 = jnp.float32
BF16 = jnp.bfloat16
PLANES = 4
CX = 128
SLOTS = 512
HALF = 256
CELLS = 512
BLK = 128
COLS = 64
GRP = 4
PANEL = 32
VMEM = pl.BlockSpec(memory_space=pltpu.VMEM)
SMEM = pl.BlockSpec(memory_space=pltpu.SMEM)


def dot(left, right):
    return jnp.dot(left, right, preferred_element_type=F32)


def dot_last(left, right):
    return lax.dot_general(left, right, (((1,), (1,)), ((), ())), preferred_element_type=F32)


def split(values):
    high = values.astype(BF16)
    low = (values - high.astype(F32)).astype(BF16)
    return high, low


def call(kernel, outs, scratch=(), limit=16, flops=0, nbytes=0):
    def run(*args):
        specs = [SMEM if a.dtype == jnp.int32 else VMEM for a in args]
        return pl.pallas_call(
            kernel,
            out_shape=[jax.ShapeDtypeStruct(s, d) for s, d in outs],
            in_specs=specs,
            out_specs=[VMEM] * len(outs),
            scratch_shapes=list(scratch),
            cost_estimate=pl.CostEstimate(flops=flops, bytes_accessed=nbytes, transcendentals=0),
            compiler_params=pltpu.CompilerParams(vmem_limit_bytes=limit << 20),
        )(*args)

    return run


def owners(g):
    even = lax.rem(g, 2) == 0
    other = jnp.where(even, g + 1, g - 1)
    return g, other, lax.rem(g + 2, GRP), GRP - 1 - g


def images_kernel(
    info, own0, own1, side0, side1, across0, across1, back0, back1, got,
    cells, images, blocks_ref, diag_ref, neart_ref, fart_ref, near_ref, far_ref,
    weights, field,
):
    g = info[0]
    live = info[1]
    even = info[2] == 0
    parts = ((own0, own1), (side0, side1), (across0, across1), (back0, back1))
    row_of = owners(g)
    rows = lax.broadcasted_iota(jnp.int32, (CX, CX), 0)
    cols = lax.broadcasted_iota(jnp.int32, (CX, CX), 1)
    gap = jnp.abs(rows - cols)
    slots = lax.broadcasted_iota(jnp.int32, (SLOTS, CX), 0)
    tri = jnp.where(gap == 0, 1.0, jnp.where(gap == 1, 0.5, 0.0)).astype(F32)
    none = jnp.zeros((CX, CX), BF16)
    weights[...] = jnp.concatenate(
        [
            jnp.concatenate([tri.astype(BF16), none], axis=1),
            jnp.concatenate([none, tri.astype(BF16)], axis=1),
        ],
        axis=0,
    )
    outer = jnp.where((g == 1) | (g == 2), 0.5, 0.0).astype(F32)
    inner = 0.5 - outer
    for p in range(PLANES):
        for o in range(GRP):
            plane = parts[o][p // 2][p % 2]
            cells[:, p * CELLS + o * CX:p * CELLS + (o + 1) * CX] = jnp.where(
                slots < live, plane[...].astype(F32), 0.0
            ).astype(BF16)
    for o in range(GRP):
        field[:, o * CX:(o + 1) * CX] = 16.0 + got[row_of[o], COLS:, :]

    def slot_half(h, carry):
        row = slice(h * HALF, (h + 1) * HALF)
        smooth = []
        for p in range(PLANES):
            low_pair = dot(cells[row, p * CELLS:p * CELLS + 2 * CX], weights[...])
            high_pair = dot(cells[row, p * CELLS + 2 * CX:(p + 1) * CELLS], weights[...])
            s0, s1 = low_pair[:, :CX], low_pair[:, CX:]
            s2, s3 = high_pair[:, :CX], high_pair[:, CX:]
            smooth.append(
                jnp.concatenate(
                    [
                        s0 + 0.5 * s1 + outer * s3,
                        s1 + 0.5 * s0 + inner * s2,
                        s2 + 0.5 * s3 + inner * s1,
                        s3 + 0.5 * s2 + outer * s0,
                    ],
                    axis=1,
                )
            )
        low_plane, high_plane = smooth[0].astype(BF16), smooth[PLANES - 1].astype(BF16)
        near_ref[row, :] = jnp.where(even, high_plane, low_plane)
        far_ref[row, :] = jnp.where(even, low_plane, high_plane)
        for p in range(PLANES):
            along = smooth[p]
            if p == 0:
                along = along + 0.5 * smooth[1]
            elif p == PLANES - 1:
                along = along + 0.5 * smooth[p - 1]
            else:
                along = along + 0.5 * (smooth[p - 1] + smooth[p + 1])
            own = cells[row, p * CELLS:(p + 1) * CELLS].astype(F32)
            images[row, p * CELLS:(p + 1) * CELLS] = (
                field[p:p + 1, :] * own - 2.0 * along
            ).astype(BF16)
        quarter = dot_last(images[row, :], cells[row, :])
        slot = lax.broadcasted_iota(jnp.int32, (HALF, HALF), 0)
        column = lax.broadcasted_iota(jnp.int32, (HALF, HALF), 1)
        pad = (slot == column) & (slot + h * HALF >= live)
        quarter = quarter + jnp.where(pad, 1.0, 0.0).astype(F32)
        diag_ref[:, row] = quarter
        for i in range(HALF // BLK):
            block = quarter[i * BLK:(i + 1) * BLK, i * BLK:(i + 1) * BLK]
            blocks_ref[:, h * HALF + i * BLK:h * HALF + (i + 1) * BLK] = 0.5 * (block + block.T)
        for c in range(GRP):
            first = (PLANES - 1) * CELLS + c * CX
            low_turned = cells[row, c * CX:(c + 1) * CX].astype(F32).T.astype(BF16)
            high_turned = cells[row, first:first + CX].astype(F32).T.astype(BF16)
            neart_ref[c * CX:(c + 1) * CX, row] = jnp.where(even, high_turned, low_turned)
            fart_ref[c * CX:(c + 1) * CX, row] = jnp.where(even, low_turned, high_turned)
        return carry

    for h in range(SLOTS // HALF):
        slot_half(h, 0)


def invert2(m):
    scale = 1.0 / (m[0] * m[3] - m[1] * m[2])
    return m[3] * scale, -(m[1] * scale), -(m[2] * scale), m[0] * scale


def times2(m, n):
    return (
        m[0] * n[0] + m[1] * n[2], m[0] * n[1] + m[1] * n[3],
        m[2] * n[0] + m[3] * n[2], m[2] * n[1] + m[3] * n[3],
    )


def invert4(m):
    a = (m[0][0], m[0][1], m[1][0], m[1][1])
    b = (m[0][2], m[0][3], m[1][2], m[1][3])
    c = (m[2][0], m[2][1], m[3][0], m[3][1])
    d = (m[2][2], m[2][3], m[3][2], m[3][3])
    ai = invert2(a)
    aib, cai = times2(ai, b), times2(c, ai)
    si = invert2(tuple(u - v for u, v in zip(d, times2(c, aib))))
    x, y = times2(aib, si), times2(si, cai)
    z = tuple(u + v for u, v in zip(ai, times2(x, cai)))
    return (
        (z[0], z[1], -x[0], -x[1]), (z[2], z[3], -x[2], -x[3]),
        (-y[0], -y[1], si[0], si[1]), (-y[2], -y[3], si[2], si[3]),
    )


def inverse_kernel(blocks_ref, diag_ref, cells, images, high_ref, low_ref, eh_ref, el_ref, work):
    work[...] = blocks_ref[...]
    lane = lax.broadcasted_iota(jnp.int32, (8, BLK), 1)
    sub = lax.broadcasted_iota(jnp.int32, (8, BLK), 0)
    base = lane - lax.rem(lane, PANEL)
    within = lax.rem(lane, PANEL)
    group = lax.div(lax.broadcasted_iota(jnp.int32, (PANEL, BLK), 1), PANEL)
    count = PANEL // 8
    panels = BLK // PANEL
    spread = lambda t, i: jnp.broadcast_to(t[i:i + 1], (8, BLK))
    turn = lambda t, n: pltpu.roll(t, (n * PANEL) % BLK, 1) if n % panels else t
    wide = lambda m, n: jnp.dot(m, n, preferred_element_type=F32, precision=lax.Precision.HIGHEST)
    for p in range(panels):
        rows = slice(p * PANEL, (p + 1) * PANEL)
        packed = None
        for j in range(GRP):
            piece = turn(work[rows, j * BLK:(j + 1) * BLK], j - p)
            packed = piece if packed is None else jnp.where(group == j, piece, packed)
        tiles = [packed[8 * v:8 * v + 8] for v in range(count)]
        lines = slice(p // 2 * HALF, (p // 2 + 1) * HALF)
        columns = slice(p % 2 * HALF, (p % 2 + 1) * HALF)
        if p // 2 == p % 2:
            matrix = diag_ref[:, columns]
        else:
            matrix = dot_last(images[lines, :], cells[columns, :])
        matrix_high, matrix_low = split(matrix)
        eh_ref[lines, columns] = matrix_high
        el_ref[lines, columns] = matrix_low
        for k in range(0, PANEL, 4):
            v, q = k // 8, k % 8
            cols = [[jnp.take_along_axis(t, base + (k + c), axis=1) for t in tiles] for c in range(4)]
            pivot = invert4([[spread(cols[c][v], q + i) for c in range(4)] for i in range(4)])
            inside = (within >= k) & (within < k + 4)
            pivot_rows = [
                jnp.where(inside, jnp.where(within == k + i, 1.0, 0.0), spread(tiles[v], q + i))
                for i in range(4)
            ]
            new = [
                (pivot[i][0] * pivot_rows[0] + pivot[i][1] * pivot_rows[1])
                + (pivot[i][2] * pivot_rows[2] + pivot[i][3] * pivot_rows[3])
                for i in range(4)
            ]
            for u in range(count):
                tile = jnp.where(inside, 0.0, tiles[u]) - (
                    (cols[0][u] * new[0] + cols[1][u] * new[1])
                    + (cols[2][u] * new[2] + cols[3][u] * new[3])
                )
                if u == v:
                    for i in range(4):
                        tile = jnp.where(sub == q + i, new[i], tile)
                tiles[u] = tile
        packed = jnp.concatenate(tiles, axis=0)
        mults = []
        for j in range(GRP):
            mult = wide(turn(packed, -j)[:, :PANEL], work[rows, j * BLK:(j + 1) * BLK])
            mults.append(jnp.where(group == p, turn(packed, p - j), mult))
        for step in range(1, panels):
            other = (p + step) % panels
            others = slice(other * PANEL, (other + 1) * PANEL)
            for j in range(GRP):
                lanes = slice(j * BLK, (j + 1) * BLK)
                block = work[others, lanes]
                change = wide(turn(block, -p)[:, :PANEL], mults[j])
                work[others, lanes] = jnp.where(group == p, 0.0, block) - change
        for j in range(GRP):
            work[rows, j * BLK:(j + 1) * BLK] = mults[j]
    high, low = split(work[...])
    high_ref[...] = high
    low_ref[...] = low


def precondition(residual, ih_ref, il_ref):
    parts = []
    for j in range(GRP):
        lanes = slice(j * BLK, (j + 1) * BLK)
        high, low = split(residual[:, lanes])
        both = dot(jnp.concatenate([high, low], axis=0), ih_ref[:, lanes])
        parts.append(both[:COLS] + both[COLS:] + dot(high, il_ref[:, lanes]))
    return DAMPING * jnp.concatenate(parts, axis=1)


def send(delta, near_ref, far_ref, near_out, far_out):
    sent = delta.astype(BF16)
    far_out[...] = dot(sent, far_ref[...]).astype(BF16)
    near_out[...] = dot(sent, near_ref[...]).astype(BF16)


def first_kernel(got, ih_ref, il_ref, near_ref, far_ref, r_ref, d_ref, near_out, far_out):
    for j in range(GRP):
        r_ref[:, j * BLK:(j + 1) * BLK] = got[j, :COLS, :]
    delta = precondition(r_ref[...], ih_ref, il_ref)
    d_ref[...] = delta
    send(delta, near_ref, far_ref, near_out, far_out)


def local_kernel(r_ref, d_ref, eh_ref, el_ref, t_ref):
    high, low = split(d_ref[...])
    both = dot(jnp.concatenate([high, low], axis=0), eh_ref[...])
    t_ref[...] = r_ref[...] - (both[:COLS] + both[COLS:] + dot(high, el_ref[...]))


def sweep_kernel(
    t_ref, far_in, near_in, neart_ref, fart_ref, ih_ref, il_ref, near_ref, far_ref,
    r_ref, d_ref, near_out, far_out,
):
    residual = t_ref[...] + dot(near_in[...], neart_ref[...]) + dot(far_in[...], fart_ref[...])
    r_ref[...] = residual
    delta = precondition(residual, ih_ref, il_ref)
    d_ref[...] = delta
    send(delta, near_ref, far_ref, near_out, far_out)


def both_kernel(r_ref, d_ref, x_ref, eh_ref, el_ref, t_ref, new_ref):
    new_ref[...] = x_ref[...] + d_ref[...]
    local_kernel(r_ref, d_ref, eh_ref, el_ref, t_ref)


def last_kernel(t_ref, x_ref, far_in, near_in, neart_ref, fart_ref, ih_ref, il_ref, out_ref):
    residual = t_ref[...] + dot(near_in[...], neart_ref[...]) + dot(far_in[...], fart_ref[...])
    out_ref[...] = x_ref[...] + precondition(residual, ih_ref, il_ref)


SIDE = ((0, 1), (1, 0), (2, 3), (3, 2))
BACK = ((0, 3), (3, 0), (1, 2), (2, 1))


def swap(values, pairs):
    return lax.ppermute(values, "grp", pairs)


def on_device_steps(deflation, shift_field, counts, right_sides):
    g = lax.axis_index("grp")
    subs = lax.axis_size("sub")
    live_count = counts[0]
    parity = lax.rem(lax.axis_index("sub"), 2)
    info = jnp.stack([g.astype(jnp.int32), live_count, parity.astype(jnp.int32)])
    planes = jnp.transpose(deflation.reshape(SLOTS, PLANES, CX), (1, 0, 2))
    own0, own1 = planes[:2], planes[2:]
    row_slot = g * BLK + lax.iota(jnp.int32, BLK)
    rhs = jnp.where((row_slot >= live_count)[:, None], 0.0, right_sides).T.reshape(GRP, COLS, BLK)
    field = jnp.zeros((8, CX), F32).at[:PLANES].set(shift_field.reshape(PLANES, CX))
    pieces = jnp.concatenate([rhs, jnp.broadcast_to(field, (GRP, 8, CX))], axis=1)
    side0 = swap(own0, SIDE)
    back1 = swap(own1, BACK)
    back0 = swap(own0, BACK)
    side1 = swap(own1, SIDE)
    across0 = swap(side0, BACK)
    across1 = swap(back1, SIDE)
    got = lax.all_to_all(pieces, "grp", 0, 0)

    square = (SLOTS, SLOTS)
    tall = (SLOTS, PLANES * CELLS)
    cells, images, blocks, diag, neart, fart, near, far = call(
        images_kernel,
        [(tall, BF16), (tall, BF16), ((BLK, SLOTS), F32), ((HALF, SLOTS), F32)]
        + [(square, BF16)] * 4,
        scratch=[pltpu.VMEM((2 * CX, 2 * CX), BF16), pltpu.VMEM((8, CELLS), F32)],
        limit=24,
        flops=2 * 10**9,
        nbytes=8 << 20,
    )(info, own0, own1, side0, side1, across0, across1, back0, back1, got)
    ih, il, eh, el = call(
        inverse_kernel,
        [((BLK, SLOTS), BF16)] * 2 + [(square, BF16)] * 2,
        scratch=[pltpu.VMEM((BLK, SLOTS), F32)],
        flops=10**9,
        nbytes=5 << 20,
    )(blocks, diag, cells, images)

    vec = (COLS, SLOTS)
    r, d, near_msg, far_msg = call(
        first_kernel, [(vec, F32), (vec, F32), (vec, BF16), (vec, BF16)],
        flops=10**8, nbytes=1 << 20,
    )(got, ih, il, near, far)
    x = d
    near_pairs = [(i, i ^ 1) for i in range(subs)]
    far_pairs = [(i, ((i + 1) ^ 1) - 1) for i in range(1, subs - 1)]
    for sweep in range(1, SWEEPS):
        far_got = lax.ppermute(far_msg, "sub", far_pairs)
        near_got = lax.ppermute(near_msg, "sub", near_pairs)
        if sweep == 1:
            (t,) = call(local_kernel, [(vec, F32)], flops=10**8, nbytes=1 << 20)(r, d, eh, el)
        else:
            t, x = call(
                both_kernel, [(vec, F32), (vec, F32)], flops=10**8, nbytes=1 << 20,
            )(r, d, x, eh, el)
        if sweep < SWEEPS - 1:
            r, d, near_msg, far_msg = call(
                sweep_kernel, [(vec, F32), (vec, F32), (vec, BF16), (vec, BF16)],
                flops=2 * 10**8, nbytes=3 << 20,
            )(t, far_got, near_got, neart, fart, ih, il, near, far)
        else:
            (x,) = call(
                last_kernel, [(vec, F32)], flops=10**8, nbytes=2 << 20,
            )(t, x, far_got, near_got, neart, fart, ih, il)
    return lax.all_to_all(x, "grp", 1, 0, tiled=True).T


def solution(mesh):
    in_specs = (
        P(None, "sub", "grp", None),
        P("sub", "grp", None),
        P("sub"),
        P(("sub", "grp"), None),
    )
    return jax.shard_map(
        on_device_steps, mesh=mesh, in_specs=in_specs,
        out_specs=P(("sub", "grp"), None), check_vma=False,
    )
```
